512 devices in a mesh: seq: 64 (over y, x, core), head: 8 (over z).
Axes of the slice: x: 4, y: 8, z: 8, core: 2. Of those that a mesh axis runs over, the one named last changes fastest.
Arguments:
- hidden_states: bfloat16 [49152, 8192], P('seq', 'head'), may hold values from -6 to 6
- k_weight: bfloat16 [8192, 1024], P('head', 'seq'), may hold values from -0.0625 to 0.0625
- v_weight: bfloat16 [8192, 1024], P('head', 'seq'), may hold values from -0.0625 to 0.0625
- assignments: int32 [8, 49152], P('head', 'seq'), may hold values from 0 to 1023
- old_centroids: float32 [8, 1024, 128], P('head'), may hold values from -6 to 6
Outputs:
- key_cache: bfloat16 [49152, 1024], P('seq', 'head')
- value_cache: bfloat16 [49152, 1024], P('seq', 'head')
- new_centroids: float32 [8, 1024, 128], P('head', 'seq')
- distances: bfloat16 [8, 49152, 1024], P('head', 'seq')
The draws below stay inside these ranges and needn't reach their ends.
All inputs are finite; a program needn't handle non-finite values.
Results may differ from the reference program's by a relative error of at most 0.017.
Values may be sent and summed in bfloat16 or wider, within the bound.
A program may use at most 64 MiB of HBM per device.

```python
import jax
import jax.numpy as jnp
from jax import lax

D = 8192
KVH = 8
HD = 128
CENT = 1024
TOKENS = 49152
FEAT_DEV = 1024
PRIOR = 48
N_HEAD = 8


def draw_hidden_states(key, part):
    noise_key = jax.random.fold_in(key, 11)
    course_key = jax.random.fold_in(key, 12)
    course = jnp.clip(jax.random.normal(course_key, (1, D), jnp.float32), -2.5, 2.5)
    position = jnp.arange(TOKENS, dtype=jnp.float32)[:, None] / TOKENS
    noise = jnp.clip(jax.random.normal(noise_key, (TOKENS, D), jnp.float32), -3.5, 3.5)
    level = 0.4 + 0.8 * position
    values = jnp.clip(noise + level * course, -6.0, 6.0)
    return values.astype(jnp.bfloat16)


def with_ends(values, key, smallest, top_value):
    index_at = [jax.random.randint(jax.random.fold_in(key, axis), (), 0, length) for axis, length in enumerate(values.shape)]
    longest = values.shape.index(max(values.shape))
    neighbour = index_at[:longest] + [(index_at[longest] + 1) % values.shape[longest]] + index_at[longest + 1:]
    return values.at[tuple(index_at)].set(smallest).at[tuple(neighbour)].set(top_value)


def level_of(own_key, dims, cuts, smallest, largest):
    def one(axis_at, parts):
        heights = jax.random.uniform(jax.random.fold_in(jax.random.fold_in(own_key, 6), axis_at), (parts,), jnp.float32, smallest / len(cuts), largest / len(cuts))
        return jnp.repeat(jnp.exp(heights), dims[axis_at] // parts).reshape((-1,) + (1,) * (len(dims) - axis_at - 1))

    gain = one(*cuts[0])
    for cut in cuts[1:]:
        gain = gain * one(*cut)
    return gain


def scatter_about(own_key, dims, scale, most, shards=(), kind=jnp.bfloat16):
    values = scale * jax.random.normal(own_key, dims, jnp.float32)
    if shards:
        values = values * level_of(own_key, dims, shards, -0.22, 0.18)
    return jnp.clip(values, -most, most).astype(kind)


def setup_inputs(seed: int = 0) -> dict:
    streams_of = jax.random.split(jax.random.key(seed), 6)
    hidden_states = draw_hidden_states(jax.random.fold_in(streams_of[5], 71), 0)
    k_weight = scatter_about(streams_of[1], (D, KVH * HD), D ** -0.5, 0.0625, ((0, 8), (1, 64)))
    v_weight = scatter_about(streams_of[2], (D, KVH * HD), D ** -0.5, 0.0625, ((0, 8), (1, 64)))
    assignments = with_ends(jax.random.randint(streams_of[3], (KVH, TOKENS), 0, CENT), jax.random.fold_in(streams_of[3], 1), 0, CENT - 1).astype(jnp.int32)
    old_centroids = scatter_about(streams_of[4], (KVH, CENT, HD), 1.0, 6.0, ((0, 8),), jnp.float32)
    return dict(hidden_states=hidden_states, k_weight=k_weight, v_weight=v_weight, assignments=assignments, old_centroids=old_centroids)


def reference(hidden_states, k_weight, v_weight, assignments, old_centroids):
    key_total = jnp.zeros((TOKENS, KVH * HD), jnp.float32)
    value_total = jnp.zeros((TOKENS, KVH * HD), jnp.float32)
    for block in range(N_HEAD):
        first_col = block * FEAT_DEV
        inputs_block = hidden_states[:, first_col:first_col + FEAT_DEV]
        key_part = jnp.dot(inputs_block, k_weight[first_col:first_col + FEAT_DEV], preferred_element_type=jnp.float32).astype(jnp.bfloat16)
        value_part = jnp.dot(inputs_block, v_weight[first_col:first_col + FEAT_DEV], preferred_element_type=jnp.float32).astype(jnp.bfloat16)
        key_part = lax.optimization_barrier(key_part)
        value_part = lax.optimization_barrier(value_part)
        key_total = key_total + key_part.astype(jnp.float32)
        value_total = value_total + value_part.astype(jnp.float32)
    key_cache = key_total.astype(jnp.bfloat16)
    value_cache = value_total.astype(jnp.bfloat16)
    key_heads = jnp.swapaxes(key_cache.reshape(TOKENS, KVH, HD), 0, 1)

    def per_head(inputs):
        assign, head_keys, previous = inputs
        onehot = (assign[:, None] == jnp.arange(CENT, dtype=jnp.int32)[None, :]).astype(jnp.bfloat16)
        sums = jnp.dot(onehot.T, head_keys, preferred_element_type=jnp.float32)
        counts = jnp.sum(onehot.astype(jnp.float32), axis=0)
        updated = (sums + PRIOR * previous) / (counts[:, None] + PRIOR)
        centroid_low = lax.optimization_barrier(updated.astype(jnp.bfloat16))
        centroid_wide = centroid_low.astype(jnp.float32)
        key_wide = head_keys.astype(jnp.float32)
        key_square = jnp.sum(key_wide * key_wide, axis=1)
        centroid_square = jnp.sum(centroid_wide * centroid_wide, axis=1)
        cross_term = jnp.dot(head_keys, centroid_low.T, preferred_element_type=jnp.float32)
        dist = (key_square[:, None] - 2.0 * cross_term + centroid_square[None, :]) / HD
        return updated, dist.astype(jnp.bfloat16)

    new_centroids, distances = lax.map(per_head, (assignments, key_heads, old_centroids))
    return key_cache, value_cache, new_centroids, distances
```

```python
import jax
import jax.numpy as jnp
from jax import lax
from jax.experimental import pallas as pl
from jax.experimental.pallas import tpu as pltpu
from jax.sharding import PartitionSpec as P

MESH = pl.DeviceIdType.MESH


def centroid_kernel(
    n, prior, sums_ref, cnt_ref, old_ref, new_ref, low_ref, got, got_cnt, low, send_sem, recv_sem
):
    me = lax.axis_index("seq")

    def peer(d):
        return {"seq": lax.rem(me + d, n)}

    barrier = pltpu.get_barrier_semaphore()

    def greet(d, c):
        pl.semaphore_signal(barrier, inc=1, device_id=peer(d), device_id_type=MESH)
        return c

    lax.fori_loop(1, n, greet, 0)
    pl.semaphore_wait(barrier, n - 1)

    def copy(src, dst, k, d):
        return pltpu.make_async_remote_copy(
            src_ref=src, dst_ref=dst, send_sem=send_sem.at[k], recv_sem=recv_sem.at[k],
            device_id=peer(d), device_id_type=MESH,
        )

    def scatter(d, c):
        to = lax.rem(me + d, n)
        copy(sums_ref.at[to], got.at[d - 1], 0, d).start()
        copy(cnt_ref.at[to], got_cnt.at[d - 1], 1, d).start()
        return c

    lax.fori_loop(1, n, scatter, 0)
    copy(got, got, 0, 1).wait_recv()
    copy(got_cnt, got_cnt, 1, 1).wait_recv()

    def add(i, c):
        return c[0] + got[i], c[1] + got_cnt[i]

    total, cnt = lax.fori_loop(0, n - 1, add, (sums_ref[me], cnt_ref[me]))
    rows = total.shape[0]
    lane = lax.broadcasted_iota(jnp.int32, (rows, 128), 1)
    row = lax.broadcasted_iota(jnp.int32, (rows, 128), 0)
    count = jnp.sum(
        jnp.where(lane == row, jnp.broadcast_to(cnt, (rows, 128)), 0.0), axis=1, keepdims=True
    )
    new = (total + prior * old_ref[...]) / (count + prior)
    new_ref[...] = new
    low[me] = new.astype(jnp.bfloat16)

    def gather(d, c):
        copy(low.at[me], low.at[me], 2, d).start()
        return c

    lax.fori_loop(1, n, gather, 0)
    rest = low.at[pl.ds(0, n - 1)]
    copy(rest, rest, 2, 1).wait_recv()
    low_ref[...] = low[...]
    copy(got, got, 0, 1).wait_send()
    copy(got_cnt, got_cnt, 1, 1).wait_send()
    copy(rest, rest, 2, 1).wait_send()


def update_centroids(sums, counts, old_own, prior):
    n, rows, width = sums.shape
    vmem = pl.BlockSpec(memory_space=pltpu.VMEM)

    def body(*refs):
        centroid_kernel(n, prior, *refs)

    return pl.pallas_call(
        body,
        name="centroids",
        out_shape=(
            jax.ShapeDtypeStruct((rows, width), jnp.float32),
            jax.ShapeDtypeStruct((n, rows, width), jnp.bfloat16),
        ),
        in_specs=[vmem] * 3,
        out_specs=(vmem, vmem),
        scratch_shapes=[
            pltpu.VMEM((n - 1, rows, width), jnp.float32),
            pltpu.VMEM((n - 1, 1, 128), jnp.float32),
            pltpu.VMEM((n, rows, width), jnp.bfloat16),
            pltpu.SemaphoreType.DMA((3,)),
            pltpu.SemaphoreType.DMA((3,)),
        ],
        compiler_params=pltpu.CompilerParams(collective_id=0, has_side_effects=True),
    )(sums, counts, old_own)


def shards(hidden_states, k_weight, v_weight, assignments, old_centroids):
    tok_rows = hidden_states.shape[0]
    clusters = old_centroids.shape[1]
    head_size = old_centroids.shape[2]
    n_seq = lax.axis_size("seq")
    stacked = jnp.stack((k_weight, v_weight), axis=1)
    partial_terms = jnp.einsum(
        "td,dkc->tkc",
        hidden_states,
        lax.all_gather(stacked, "seq", axis=2, tiled=True),
        preferred_element_type=jnp.float32,
    )
    summed = lax.psum_scatter(
        partial_terms.astype(jnp.bfloat16), "head", scatter_dimension=2, tiled=True
    ).astype(jnp.float32)
    keys = summed[:, 0].astype(jnp.bfloat16)
    value_cache = summed[:, 1].astype(jnp.bfloat16)
    onehot = assignments[0][:, None] == jnp.arange(clusters, dtype=jnp.int32)[None, :]
    local_sums = jnp.einsum(
        "tc,te->ce", onehot.astype(jnp.bfloat16), keys, preferred_element_type=jnp.float32
    )
    local_counts = jnp.sum(onehot.astype(jnp.float32), axis=0)
    prior_weight = float(tok_rows * n_seq // clusters)
    share = clusters // n_seq
    counts = jnp.pad(local_counts.reshape(n_seq, 1, share), ((0, 0), (0, 0), (0, 128 - share)))
    old_own = lax.dynamic_slice_in_dim(old_centroids[0], lax.axis_index("seq") * share, share, 0)
    new_own, low = update_centroids(
        local_sums.reshape(n_seq, share, head_size), counts, old_own, prior_weight
    )
    low = low.reshape(clusters, head_size)
    wide = low.astype(jnp.float32)
    centroid_square = jnp.sum(wide * wide, axis=1)
    key_wide = keys.astype(jnp.float32)
    key_square = jnp.sum(key_wide * key_wide, axis=1)
    cross_term = jnp.einsum("te,ce->tc", keys, low, preferred_element_type=jnp.float32)
    dist = (key_square[:, None] - 2.0 * cross_term + centroid_square[None, :]) / head_size
    return (keys, value_cache, new_own[None], dist.astype(jnp.bfloat16)[None])


def solution(mesh):
    in_specs = (
        P("seq", "head"),
        P("head", "seq"),
        P("head", "seq"),
        P("head", "seq"),
        P("head", None, None),
    )
    out_specs = (P("seq", "head"), P("seq", "head"), P("head", "seq", None), P("head", "seq", None))
    return jax.shard_map(shards, mesh=mesh, in_specs=in_specs, out_specs=out_specs, check_vma=False)
```

```python
import jax
import jax.numpy as jnp
from jax import lax
from jax.experimental import pallas as pl
from jax.experimental.pallas import tpu as pltpu
from jax.sharding import PartitionSpec as P

MESH = pl.DeviceIdType.MESH
NX, NY, NZ = 4, 8, 8
PIECES = 2


def centroid_kernel(
    n, prior, sums_ref, cnt_ref, old_ref, new_ref, low_ref, got, got_cnt, low, send_sem, recv_sem
):
    me = lax.axis_index("seq")

    def peer(d):
        return {"seq": lax.rem(me + d, n)}

    barrier = pltpu.get_barrier_semaphore()

    def greet(d, c):
        pl.semaphore_signal(barrier, inc=1, device_id=peer(d), device_id_type=MESH)
        return c

    lax.fori_loop(1, n, greet, 0)
    pl.semaphore_wait(barrier, n - 1)

    def copy(src, dst, k, d):
        return pltpu.make_async_remote_copy(
            src_ref=src, dst_ref=dst, send_sem=send_sem.at[k], recv_sem=recv_sem.at[k],
            device_id=peer(d), device_id_type=MESH,
        )

    def scatter(d, c):
        to = lax.rem(me + d, n)
        copy(sums_ref.at[to], got.at[d - 1], 0, d).start()
        copy(cnt_ref.at[to], got_cnt.at[d - 1], 1, d).start()
        return c

    lax.fori_loop(1, n, scatter, 0)
    copy(got, got, 0, 1).wait_recv()
    copy(got_cnt, got_cnt, 1, 1).wait_recv()

    def add(i, c):
        return c[0] + got[i], c[1] + got_cnt[i]

    total, cnt = lax.fori_loop(0, n - 1, add, (sums_ref[me], cnt_ref[me]))
    rows = total.shape[0]
    lane = lax.broadcasted_iota(jnp.int32, (rows, 128), 1)
    row = lax.broadcasted_iota(jnp.int32, (rows, 128), 0)
    count = jnp.sum(
        jnp.where(lane == row, jnp.broadcast_to(cnt, (rows, 128)), 0.0), axis=1, keepdims=True
    )
    new = (total + prior * old_ref[...]) / (count + prior)
    new_ref[...] = new
    low[me] = new.astype(jnp.bfloat16)

    def gather(d, c):
        copy(low.at[me], low.at[me], 2, d).start()
        return c

    lax.fori_loop(1, n, gather, 0)
    rest = low.at[pl.ds(0, n - 1)]
    copy(rest, rest, 2, 1).wait_recv()
    low_ref[...] = low[...]
    copy(got, got, 0, 1).wait_send()
    copy(got_cnt, got_cnt, 1, 1).wait_send()
    copy(rest, rest, 2, 1).wait_send()


def update_centroids(sums, counts, old_own, prior):
    n, rows, width = sums.shape
    vmem = pl.BlockSpec(memory_space=pltpu.VMEM)

    def body(*refs):
        centroid_kernel(n, prior, *refs)

    return pl.pallas_call(
        body,
        name="centroids",
        out_shape=(
            jax.ShapeDtypeStruct((rows, width), jnp.float32),
            jax.ShapeDtypeStruct((n, rows, width), jnp.bfloat16),
        ),
        in_specs=[vmem] * 3,
        out_specs=(vmem, vmem),
        scratch_shapes=[
            pltpu.VMEM((n - 1, rows, width), jnp.float32),
            pltpu.VMEM((n - 1, 1, 128), jnp.float32),
            pltpu.VMEM((n, rows, width), jnp.bfloat16),
            pltpu.SemaphoreType.DMA((3,)),
            pltpu.SemaphoreType.DMA((3,)),
        ],
        compiler_params=pltpu.CompilerParams(collective_id=0, has_side_effects=True),
    )(sums, counts, old_own)


def project_kernel(h_ref, w_ref, k_ref, v_ref, held, part, plus, minus, send, recv, zsend, zrecv):
    me = lax.axis_index("seq")
    z = lax.axis_index("head")
    core = lax.rem(me, 2)
    x = lax.rem(me // 2, NX)
    y = me // (2 * NX)

    def at(y_, x_, core_):
        return {"seq": (lax.rem(y_, NY) * NX + lax.rem(x_, NX)) * 2 + core_}

    above, below = at(y + 1, x, core), at(y + NY - 1, x, core)
    partner = at(y, x, 1 - core)
    z_up, z_down = {"head": lax.rem(z + 1, NZ)}, {"head": lax.rem(z + NZ - 1, NZ)}
    x_peers = [at(y, x + NX - k, core) for k in range(1, NX)]

    barrier = pltpu.get_barrier_semaphore()
    peers = [above, below, partner, z_up, z_down] + x_peers
    for peer in peers:
        pl.semaphore_signal(barrier, inc=1, device_id=peer, device_id_type=MESH)
    pl.semaphore_wait(barrier, len(peers))

    sent = []

    def block(row, k, c=core):
        return held.at[lax.rem(row, NY), c, lax.rem(x + k, NX)]

    def copy(ref, i, to):
        return pltpu.make_async_remote_copy(
            src_ref=ref, dst_ref=ref, send_sem=send.at[i], recv_sem=recv.at[i],
            device_id=to, device_id_type=MESH,
        )

    def push(ref, i, to):
        c = copy(ref, i, to)
        c.start()
        sent.append(c)

    def up(s, k):
        return (s - 1) * NX + k

    def down(s, k):
        return 16 + (s - 1) * NX + k

    def side(i):
        return 36 + i

    own = pltpu.make_async_copy(w_ref, block(y, 0), send.at[72])
    own.start()
    own.wait()
    for k in range(1, NX):
        ref = block(y, 0)
        push(ref, 68 + k, x_peers[k - 1])
    for k in range(NX):
        ref = block(y, k)
        if k:
            copy(ref, 68 + k, partner).wait_recv()
        push(ref, up(1, k), above)
        push(ref, down(1, k), below)
        push(ref, 32 + k, partner)

    def project(row):
        head = lax.rem(row, NY)
        weights = jnp.concatenate(
            [held[head, c, i, j] for j in range(2) for i in range(NX) for c in range(2)], axis=0
        )

        def rows(i, carry):
            at_rows = pl.ds(pl.multiple_of(i * 256, 256), 256)
            out = lax.dot_general(
                h_ref[at_rows, :], weights, (((1,), (1,)), ((), ())),
                preferred_element_type=jnp.float32,
            ).astype(jnp.bfloat16)
            part[head, 0, at_rows, :] = out[:, :128]
            part[head, 1, at_rows, :] = out[:, 128:]
            return carry

        lax.fori_loop(0, h_ref.shape[0] // 256, rows, 0)

    for k in range(NX):
        copy(block(y, k, 1 - core), 32 + k, partner).wait_recv()
    project(y)
    half = NY // 2
    for s in range(1, half + 1):
        ups = [k for k in range(NX) if s < half or k < NX // 2]
        downs = [k for k in range(NX) if s < half or k >= NX // 2]
        for k in range(NX):
            if k in ups:
                ref = block(y + NY - s, k)
                copy(ref, up(s, k), partner).wait_recv()
                if s < half - 1 or (s == half - 1 and k < NX // 2):
                    push(ref, up(s + 1, k), above)
                push(ref, side(up(s, k)), partner)
            if k in downs:
                ref = block(y + s, k)
                copy(ref, down(s, k), partner).wait_recv()
                if s < half - 1 or (s == half - 1 and k >= NX // 2):
                    push(ref, down(s + 1, k), below)
                push(ref, side(down(s, k)), partner)
        for k in ups:
            copy(block(y + NY - s, k, 1 - core), side(up(s, k)), partner).wait_recv()
        if s < half:
            project(y + NY - s)
        for k in downs:
            copy(block(y + s, k, 1 - core), side(down(s, k)), partner).wait_recv()
        project(y + s)

    tall = h_ref.shape[0] // PIECES

    def ring(src, dst, i, to):
        c = pltpu.make_async_remote_copy(
            src_ref=src, dst_ref=dst, send_sem=zsend.at[i], recv_sem=zrecv.at[i],
            device_id=to, device_id_type=MESH,
        )
        return c

    def ring_push(src, dst, i, to):
        c = ring(src, dst, i, to)
        c.start()
        sent.append(c)

    ways = ((0, plus, z_up, NZ - 1, k_ref), (1, minus, z_down, 1, v_ref))
    for p in range(PIECES):
        rows = pl.ds(p * tall, tall)
        for j, slots, to, step, _ in ways:
            src = part.at[lax.rem(z + step, NZ), j, rows]
            ring_push(src, slots.at[0, rows], (j * (NZ - 1)) * PIECES + p, to)
    for s in range(NZ - 1):
        for p in range(PIECES):
            rows = pl.ds(p * tall, tall)
            for j, slots, to, step, out in ways:
                i = (j * (NZ - 1) + s) * PIECES + p
                here = slots.at[s, rows]
                ring(here, here, i, to).wait_recv()
                head = lax.rem(z + step * (s + 2), NZ)
                total = slots[s, rows].astype(jnp.float32) + part[head, j, rows].astype(jnp.float32)
                total = total.astype(jnp.bfloat16)
                if s < NZ - 2:
                    slots[s, rows] = total
                    ring_push(here, slots.at[s + 1, rows], i + PIECES, to)
                else:
                    out[rows, :] = total
    for c in sent:
        c.wait_send()


def project_keys(hidden, weights):
    tok_rows = hidden.shape[0]
    vmem = pl.BlockSpec(memory_space=pltpu.VMEM)
    out = jax.ShapeDtypeStruct((tok_rows, 128), jnp.bfloat16)
    n_ring = 2 * (NZ - 1) * PIECES
    return pl.pallas_call(
        project_kernel,
        name="project",
        out_shape=(out, out),
        in_specs=[vmem] * 2,
        out_specs=(vmem, vmem),
        scratch_shapes=[
            pltpu.VMEM((NY, 2, NX) + weights.shape, jnp.bfloat16),
            pltpu.VMEM((NZ, 2, tok_rows, 128), jnp.bfloat16),
            pltpu.VMEM((NZ - 1, tok_rows, 128), jnp.bfloat16),
            pltpu.VMEM((NZ - 1, tok_rows, 128), jnp.bfloat16),
            pltpu.SemaphoreType.DMA((73,)),
            pltpu.SemaphoreType.DMA((73,)),
            pltpu.SemaphoreType.DMA((n_ring,)),
            pltpu.SemaphoreType.DMA((n_ring,)),
        ],
        compiler_params=pltpu.CompilerParams(collective_id=1, has_side_effects=True),
    )(hidden, weights)


def shards(hidden_states, k_weight, v_weight, assignments, old_centroids):
    tok_rows = hidden_states.shape[0]
    clusters = old_centroids.shape[1]
    head_size = old_centroids.shape[2]
    n_seq = lax.axis_size("seq")
    weights = jnp.stack((k_weight.T, v_weight.T), axis=0)
    keys, value_cache = project_keys(hidden_states, weights)
    onehot = assignments[0][:, None] == jnp.arange(clusters, dtype=jnp.int32)[None, :]
    local_sums = jnp.einsum(
        "tc,te->ce", onehot.astype(jnp.bfloat16), keys, preferred_element_type=jnp.float32
    )
    local_counts = jnp.sum(onehot.astype(jnp.float32), axis=0)
    prior_weight = float(tok_rows * n_seq // clusters)
    share = clusters // n_seq
    counts = jnp.pad(local_counts.reshape(n_seq, 1, share), ((0, 0), (0, 0), (0, 128 - share)))
    old_own = lax.dynamic_slice_in_dim(old_centroids[0], lax.axis_index("seq") * share, share, 0)
    new_own, low = update_centroids(
        local_sums.reshape(n_seq, share, head_size), counts, old_own, prior_weight
    )
    low = low.reshape(clusters, head_size)
    wide = low.astype(jnp.float32)
    centroid_square = jnp.sum(wide * wide, axis=1)
    key_wide = keys.astype(jnp.float32)
    key_square = jnp.sum(key_wide * key_wide, axis=1)
    cross_term = jnp.einsum("te,ce->tc", keys, low, preferred_element_type=jnp.float32)
    dist = (key_square[:, None] - 2.0 * cross_term + centroid_square[None, :]) / head_size
    return (keys, value_cache, new_own[None], dist.astype(jnp.bfloat16)[None])


def solution(mesh):
    in_specs = (
        P("seq", "head"),
        P("head", "seq"),
        P("head", "seq"),
        P("head", "seq"),
        P("head", None, None),
    )
    out_specs = (P("seq", "head"), P("seq", "head"), P("head", "seq", None), P("head", "seq", None))
    return jax.shard_map(shards, mesh=mesh, in_specs=in_specs, out_specs=out_specs, check_vma=False)
```

```python
import jax
import jax.numpy as jnp
from jax import lax
from jax.experimental import pallas as pl
from jax.experimental.pallas import tpu as pltpu
from jax.sharding import PartitionSpec as P

MESH = pl.DeviceIdType.MESH
NX, NY, NZ = 4, 8, 8
CHIPS = NX * NY
PIECES = 2


def remote(src, dst, send_sem, recv_sem, to):
    return pltpu.make_async_remote_copy(
        src_ref=src, dst_ref=dst, send_sem=send_sem, recv_sem=recv_sem,
        device_id=to, device_id_type=MESH,
    )


def z_neighbours():
    z = lax.axis_index("head")
    return {"head": lax.rem(z + 1, NZ)}, {"head": lax.rem(z + NZ - 1, NZ)}


class Ring:
    def __init__(self, part, out, plus, minus, send, recv, sent):
        self.part, self.out, self.send, self.recv, self.sent = part, out, send, recv, sent
        self.z = lax.axis_index("head")
        up, down = z_neighbours()
        self.half = out.shape[0] // 2
        self.tall = self.half // PIECES
        self.ways = ((0, plus, up, NZ - 1), (1, minus, down, 1))

    def copy(self, src, dst, i, to):
        return remote(src, dst, self.send.at[i], self.recv.at[i], to)

    def push(self, src, dst, i, to):
        c = self.copy(src, dst, i, to)
        c.start()
        self.sent.append(c)

    def start(self):
        for p in range(PIECES):
            for j, slots, to, step in self.ways:
                src = self.part.at[
                    lax.rem(self.z + step, NZ), pl.ds(j * self.half + p * self.tall, self.tall)
                ]
                dst = slots.at[0, pl.ds(p * self.tall, self.tall)]
                self.push(src, dst, j * (NZ - 1) * PIECES + p, to)

    def step(self, s):
        for p in range(PIECES):
            rows = pl.ds(p * self.tall, self.tall)
            for j, slots, to, step in self.ways:
                i = (j * (NZ - 1) + s) * PIECES + p
                here = slots.at[s, rows]
                full = pl.ds(j * self.half + p * self.tall, self.tall)
                self.copy(here, here, i, to).wait_recv()
                head = lax.rem(self.z + step * (s + 2), NZ)
                total = slots[s, rows].astype(jnp.float32) + self.part[head, full].astype(jnp.float32)
                total = total.astype(jnp.bfloat16)
                if s < NZ - 2:
                    slots[s, rows] = total
                    self.push(here, slots.at[s + 1, rows], i + PIECES, to)
                else:
                    self.out[full, :] = total


def ring_scratch(tok_rows):
    n_ring = 2 * (NZ - 1) * PIECES
    return [
        pltpu.VMEM((NZ - 1, tok_rows // 2, 128), jnp.bfloat16),
        pltpu.VMEM((NZ - 1, tok_rows // 2, 128), jnp.bfloat16),
        pltpu.SemaphoreType.DMA((n_ring,)),
        pltpu.SemaphoreType.DMA((n_ring,)),
    ]


def enter(peers, chips=None):
    barrier = pltpu.get_barrier_semaphore()
    for peer in peers:
        pl.semaphore_signal(barrier, inc=1, device_id=peer, device_id_type=MESH)
    count = len(peers)
    if chips is not None:

        def greet(d, c):
            pl.semaphore_signal(barrier, inc=1, device_id=chips(d), device_id_type=MESH)
            return c

        lax.fori_loop(1, CHIPS, greet, 0)
        count += CHIPS - 1
    pl.semaphore_wait(barrier, count)


def project_kernel(
    h_ref, w_ref, k_ref, pv_ref, held, pk, send, recv, own_sem, plus, minus, zsend, zrecv
):
    me = lax.axis_index("seq")
    core = lax.rem(me, 2)
    x = lax.rem(me // 2, NX)
    y = me // (2 * NX)

    def at(y_, x_, core_):
        return {"seq": (lax.rem(y_, NY) * NX + lax.rem(x_, NX)) * 2 + core_}

    above, below = at(y + 1, x, core), at(y + NY - 1, x, core)
    partner = at(y, x, 1 - core)
    z_up, z_down = z_neighbours()
    x_peers = [at(y, x + NX - k, core) for k in range(1, NX)]
    enter([above, below, partner, z_up, z_down] + x_peers)

    sent = []
    parts = (pk, pv_ref)

    def block(j, row, k, c=core):
        return held.at[j, lax.rem(row, NY), c, lax.rem(x + k, NX)]

    def copy(j, ref, i, to):
        return remote(ref, ref, send.at[j, i], recv.at[j, i], to)

    def push(j, ref, i, to):
        c = copy(j, ref, i, to)
        c.start()
        sent.append(c)

    def up(s, k):
        return (s - 1) * NX + k

    def down(s, k):
        return 16 + (s - 1) * NX + k

    def side(i):
        return 36 + i

    def project(j, rows_y):
        heads = [lax.rem(row, NY) for row in rows_y]
        weights = jnp.concatenate(
            [held[j, head, c, i] for head in heads for i in range(NX) for c in range(2)], axis=0
        )

        def rows(i, carry):
            at_rows = pl.ds(pl.multiple_of(i * 256, 256), 256)
            out = lax.dot_general(
                h_ref[at_rows, :], weights, (((1,), (1,)), ((), ())),
                preferred_element_type=jnp.float32,
            ).astype(jnp.bfloat16)
            for q, head in enumerate(heads):
                parts[j][head, at_rows, :] = out[:, q * 128:(q + 1) * 128]
            return carry

        lax.fori_loop(0, h_ref.shape[0] // 256, rows, 0)

    def first(j):
        for k in range(NX):
            ref = block(j, y, k)
            if k:
                copy(j, ref, 68 + k, partner).wait_recv()
            push(j, ref, up(1, k), above)
            push(j, ref, down(1, k), below)
            push(j, ref, 32 + k, partner)

    def mine(j):
        for k in range(NX):
            copy(j, block(j, y, k, 1 - core), 32 + k, partner).wait_recv()
        project(j, [y])

    half = NY // 2

    def relay(j, s):
        ups = [k for k in range(NX) if s < half or k < NX // 2]
        downs = [k for k in range(NX) if s < half or k >= NX // 2]
        for k in range(NX):
            if k in ups:
                ref = block(j, y + NY - s, k)
                copy(j, ref, up(s, k), partner).wait_recv()
                if s < half - 1 or (s == half - 1 and k < NX // 2):
                    push(j, ref, up(s + 1, k), above)
                push(j, ref, side(up(s, k)), partner)
            if k in downs:
                ref = block(j, y + s, k)
                copy(j, ref, down(s, k), partner).wait_recv()
                if s < half - 1 or (s == half - 1 and k >= NX // 2):
                    push(j, ref, down(s + 1, k), below)
                push(j, ref, side(down(s, k)), partner)
        for k in ups:
            copy(j, block(j, y + NY - s, k, 1 - core), side(up(s, k)), partner).wait_recv()
        for k in downs:
            copy(j, block(j, y + s, k, 1 - core), side(down(s, k)), partner).wait_recv()
        project(j, [y + NY - s, y + s] if s < half else [y + s])

    own = [
        pltpu.make_async_copy(w_ref.at[j], block(j, y, 0), own_sem.at[j]) for j in range(2)
    ]
    for j in range(2):
        own[j].start()
    for j in range(2):
        own[j].wait()
        for k in range(1, NX):
            push(j, block(j, y, 0), 68 + k, x_peers[k - 1])
    first(0)
    mine(0)
    for s in range(1, half + 1):
        relay(0, s)
    ring = Ring(pk, k_ref, plus, minus, zsend, zrecv, sent)
    ring.start()
    first(1)
    mine(1)
    for s in range(NZ - 1):
        ring.step(s)
        if s in (0, 2, 4, 5):
            relay(1, (0, 2, 4, 5).index(s) + 1)
    for c in sent:
        c.wait_send()


def project_keys(hidden, weights):
    tok_rows = hidden.shape[0]
    vmem = pl.BlockSpec(memory_space=pltpu.VMEM)
    return pl.pallas_call(
        project_kernel,
        name="project",
        out_shape=(
            jax.ShapeDtypeStruct((tok_rows, 128), jnp.bfloat16),
            jax.ShapeDtypeStruct((NZ, tok_rows, 128), jnp.bfloat16),
        ),
        in_specs=[vmem] * 2,
        out_specs=(vmem, vmem),
        scratch_shapes=[
            pltpu.VMEM((2, NY, 2, NX) + weights.shape[1:], jnp.bfloat16),
            pltpu.VMEM((NZ, tok_rows, 128), jnp.bfloat16),
            pltpu.SemaphoreType.DMA((2, 72)),
            pltpu.SemaphoreType.DMA((2, 72)),
            pltpu.SemaphoreType.DMA((2,)),
        ] + ring_scratch(tok_rows),
        compiler_params=pltpu.CompilerParams(collective_id=1, has_side_effects=True),
    )(hidden, weights)


def centroid_kernel(
    prior, sums_ref, cnt_ref, old_ref, pv_ref, new_ref, low_ref, v_ref,
    pair, pair_cnt, mix, mix_cnt, got, got_cnt, low, send, recv, plus, minus, zsend, zrecv
):
    me = lax.axis_index("seq")
    core = lax.rem(me, 2)
    chip = me // 2
    partner = {"seq": chip * 2 + 1 - core}
    z_up, z_down = z_neighbours()

    def peer(d):
        return {"seq": lax.rem(chip + d, CHIPS) * 2 + core}

    enter([partner, z_up, z_down], peer)

    def copy(src, dst, k, to):
        return remote(src, dst, send.at[k], recv.at[k], to)

    sent = []
    ring = Ring(pv_ref, v_ref, plus, minus, zsend, zrecv, sent)
    to_pair = copy(sums_ref.at[:, 1 - core], pair, 0, partner)
    to_pair_cnt = copy(cnt_ref.at[:, 1 - core], pair_cnt, 1, partner)
    to_pair.start()
    to_pair_cnt.start()
    ring.start()
    to_pair.wait_recv()
    to_pair_cnt.wait_recv()

    def merge(i, c):
        mix[i] = sums_ref[i, core] + pair[i]
        mix_cnt[i] = cnt_ref[i, core] + pair_cnt[i]
        return c

    lax.fori_loop(0, CHIPS, merge, 0)

    def scatter(d, c):
        to = lax.rem(chip + d, CHIPS)
        copy(mix.at[to], got.at[d - 1], 2, peer(d)).start()
        copy(mix_cnt.at[to], got_cnt.at[d - 1], 3, peer(d)).start()
        return c

    lax.fori_loop(1, CHIPS, scatter, 0)
    for s in range(3):
        ring.step(s)
    copy(got, got, 2, partner).wait_recv()
    copy(got_cnt, got_cnt, 3, partner).wait_recv()

    def add(i, c):
        return c[0] + got[i], c[1] + got_cnt[i]

    total, cnt = lax.fori_loop(0, CHIPS - 1, add, (mix[chip], mix_cnt[chip]))
    rows = total.shape[0]
    lane = lax.broadcasted_iota(jnp.int32, (rows, 128), 1)
    row = lax.broadcasted_iota(jnp.int32, (rows, 128), 0)
    count = jnp.sum(
        jnp.where(lane == row, jnp.broadcast_to(cnt, (rows, 128)), 0.0), axis=1, keepdims=True
    )
    new = (total + prior * old_ref[...]) / (count + prior)
    new_ref[...] = new
    low[core, chip] = new.astype(jnp.bfloat16)

    def gather(d, c):
        copy(low.at[core, chip], low.at[core, chip], 4, peer(d)).start()
        return c

    lax.fori_loop(1, CHIPS, gather, 0)
    for s in range(3, 6):
        ring.step(s)
    rest = low.at[core, pl.ds(0, CHIPS - 1)]
    copy(rest, rest, 4, partner).wait_recv()
    back = copy(low.at[core], low.at[core], 5, partner)
    back.start()
    ring.step(6)
    back.wait_recv()
    low_ref[:, 0] = low[0]
    low_ref[:, 1] = low[1]
    to_pair.wait_send()
    to_pair_cnt.wait_send()
    copy(got, got, 2, partner).wait_send()
    copy(got_cnt, got_cnt, 3, partner).wait_send()
    copy(rest, rest, 4, partner).wait_send()
    back.wait_send()
    for c in sent:
        c.wait_send()


def update_centroids(sums, counts, old_own, part_v, prior):
    rows, width = old_own.shape
    tok_rows = part_v.shape[1]
    vmem = pl.BlockSpec(memory_space=pltpu.VMEM)

    def body(*refs):
        centroid_kernel(prior, *refs)

    return pl.pallas_call(
        body,
        name="centroids",
        out_shape=(
            jax.ShapeDtypeStruct((rows, width), jnp.float32),
            jax.ShapeDtypeStruct((CHIPS, 2, rows, width), jnp.bfloat16),
            jax.ShapeDtypeStruct((tok_rows, 128), jnp.bfloat16),
        ),
        in_specs=[vmem] * 4,
        out_specs=(vmem, vmem, vmem),
        scratch_shapes=[
            pltpu.VMEM((CHIPS, rows, width), jnp.float32),
            pltpu.VMEM((CHIPS, 1, 128), jnp.float32),
            pltpu.VMEM((CHIPS, rows, width), jnp.float32),
            pltpu.VMEM((CHIPS, 1, 128), jnp.float32),
            pltpu.VMEM((CHIPS - 1, rows, width), jnp.float32),
            pltpu.VMEM((CHIPS - 1, 1, 128), jnp.float32),
            pltpu.VMEM((2, CHIPS, rows, width), jnp.bfloat16),
            pltpu.SemaphoreType.DMA((6,)),
            pltpu.SemaphoreType.DMA((6,)),
        ] + ring_scratch(tok_rows),
        compiler_params=pltpu.CompilerParams(collective_id=0, has_side_effects=True),
    )(sums, counts, old_own, part_v)


def shards(hidden_states, k_weight, v_weight, assignments, old_centroids):
    tok_rows = hidden_states.shape[0]
    clusters = old_centroids.shape[1]
    head_size = old_centroids.shape[2]
    n_seq = lax.axis_size("seq")
    weights = jnp.stack((k_weight.T, v_weight.T), axis=0)
    keys, part_v = project_keys(hidden_states, weights)
    onehot = assignments[0][:, None] == jnp.arange(clusters, dtype=jnp.int32)[None, :]
    local_sums = jnp.einsum(
        "tc,te->ce", onehot.astype(jnp.bfloat16), keys, preferred_element_type=jnp.float32
    )
    local_counts = jnp.sum(onehot.astype(jnp.float32), axis=0)
    prior_weight = float(tok_rows * n_seq // clusters)
    share = clusters // n_seq
    counts = jnp.pad(
        local_counts.reshape(CHIPS, 2, 1, share), ((0, 0), (0, 0), (0, 0), (0, 128 - share))
    )
    old_own = lax.dynamic_slice_in_dim(old_centroids[0], lax.axis_index("seq") * share, share, 0)
    new_own, low, value_cache = update_centroids(
        local_sums.reshape(CHIPS, 2, share, head_size), counts, old_own, part_v, prior_weight
    )
    low = low.reshape(clusters, head_size)
    wide = low.astype(jnp.float32)
    centroid_square = jnp.sum(wide * wide, axis=1)
    key_wide = keys.astype(jnp.float32)
    key_square = jnp.sum(key_wide * key_wide, axis=1)
    cross_term = jnp.einsum("te,ce->tc", keys, low, preferred_element_type=jnp.float32)
    dist = (key_square[:, None] - 2.0 * cross_term + centroid_square[None, :]) / head_size
    return (keys, value_cache, new_own[None], dist.astype(jnp.bfloat16)[None])


def solution(mesh):
    in_specs = (
        P("seq", "head"),
        P("head", "seq"),
        P("head", "seq"),
        P("head", "seq"),
        P("head", None, None),
    )
    out_specs = (P("seq", "head"), P("seq", "head"), P("head", "seq", None), P("head", "seq", None))
    return jax.shard_map(shards, mesh=mesh, in_specs=in_specs, out_specs=out_specs, check_vma=False)
```

```python
import jax
import jax.numpy as jnp
from jax import lax
from jax.experimental import pallas as pl
from jax.experimental.pallas import tpu as pltpu
from jax.sharding import PartitionSpec as P

MESH = pl.DeviceIdType.MESH
NX, NY, NZ = 4, 8, 8
CHIPS = NX * NY
PIECES = 3


def remote(src, dst, send_sem, recv_sem, to):
    return pltpu.make_async_remote_copy(
        src_ref=src, dst_ref=dst, send_sem=send_sem, recv_sem=recv_sem,
        device_id=to, device_id_type=MESH,
    )


def z_neighbours():
    z = lax.axis_index("head")
    return {"head": lax.rem(z + 1, NZ)}, {"head": lax.rem(z + NZ - 1, NZ)}


class Ring:
    def __init__(self, part, out, plus, minus, send, recv, sent):
        self.part, self.out, self.send, self.recv, self.sent = part, out, send, recv, sent
        self.z = lax.axis_index("head")
        up, down = z_neighbours()
        self.half = out.shape[0] // 2
        self.tall = self.half // PIECES
        self.ways = ((0, plus, up, NZ - 1), (1, minus, down, 1))

    def copy(self, src, dst, i, to):
        return remote(src, dst, self.send.at[i], self.recv.at[i], to)

    def push(self, src, dst, i, to):
        c = self.copy(src, dst, i, to)
        c.start()
        self.sent.append(c)

    def start(self):
        for p in range(PIECES):
            for j, slots, to, step in self.ways:
                src = self.part.at[
                    lax.rem(self.z + step, NZ), pl.ds(j * self.half + p * self.tall, self.tall)
                ]
                dst = slots.at[0, pl.ds(p * self.tall, self.tall)]
                self.push(src, dst, j * (NZ - 1) * PIECES + p, to)

    def step(self, s):
        for p in range(PIECES):
            rows = pl.ds(p * self.tall, self.tall)
            for j, slots, to, step in self.ways:
                i = (j * (NZ - 1) + s) * PIECES + p
                here = slots.at[s, rows]
                full = pl.ds(j * self.half + p * self.tall, self.tall)
                self.copy(here, here, i, to).wait_recv()
                head = lax.rem(self.z + step * (s + 2), NZ)
                total = slots[s, rows].astype(jnp.float32) + self.part[head, full].astype(jnp.float32)
                total = total.astype(jnp.bfloat16)
                if s < NZ - 2:
                    slots[s, rows] = total
                    self.push(here, slots.at[s + 1, rows], i + PIECES, to)
                else:
                    self.out[full, :] = total


def ring_scratch(tok_rows):
    n_ring = 2 * (NZ - 1) * PIECES
    return [
        pltpu.VMEM((NZ - 1, tok_rows // 2, 128), jnp.bfloat16),
        pltpu.VMEM((NZ - 1, tok_rows // 2, 128), jnp.bfloat16),
        pltpu.SemaphoreType.DMA((n_ring,)),
        pltpu.SemaphoreType.DMA((n_ring,)),
    ]


def enter(peers, chips=None):
    barrier = pltpu.get_barrier_semaphore()
    for peer in peers:
        pl.semaphore_signal(barrier, inc=1, device_id=peer, device_id_type=MESH)
    count = len(peers)
    if chips is not None:

        def greet(d, c):
            pl.semaphore_signal(barrier, inc=1, device_id=chips(d), device_id_type=MESH)
            return c

        lax.fori_loop(1, CHIPS, greet, 0)
        count += CHIPS - 1
    pl.semaphore_wait(barrier, count)


def project_kernel(
    h_ref, w_ref, k_ref, pv_ref, held, pk, send, recv, own_sem, plus, minus, zsend, zrecv
):
    me = lax.axis_index("seq")
    core = lax.rem(me, 2)
    x = lax.rem(me // 2, NX)
    y = me // (2 * NX)

    def at(y_, x_, core_):
        return {"seq": (lax.rem(y_, NY) * NX + lax.rem(x_, NX)) * 2 + core_}

    above, below = at(y + 1, x, core), at(y + NY - 1, x, core)
    partner = at(y, x, 1 - core)
    z_up, z_down = z_neighbours()
    x_peers = [at(y, x + NX - k, core) for k in range(1, NX)]
    enter([above, below, partner, z_up, z_down] + x_peers)

    sent = []
    parts = (pk, pv_ref)

    def block(j, row, k, c=core):
        return held.at[j, lax.rem(row, NY), c, lax.rem(x + k, NX)]

    def copy(j, ref, i, to):
        return remote(ref, ref, send.at[j, i], recv.at[j, i], to)

    def push(j, ref, i, to):
        c = copy(j, ref, i, to)
        c.start()
        sent.append(c)

    def up(s, k):
        return (s - 1) * NX + k

    def down(s, k):
        return 16 + (s - 1) * NX + k

    def side(i):
        return 36 + i

    def project(j, rows_y):
        heads = [lax.rem(row, NY) for row in rows_y]
        weights = jnp.concatenate(
            [held[j, head, c, i] for head in heads for i in range(NX) for c in range(2)], axis=0
        )

        def rows(i, carry):
            at_rows = pl.ds(pl.multiple_of(i * 384, 384), 384)
            out = lax.dot_general(
                h_ref[at_rows, :], weights, (((1,), (1,)), ((), ())),
                preferred_element_type=jnp.float32,
            ).astype(jnp.bfloat16)
            for q, head in enumerate(heads):
                parts[j][head, at_rows, :] = out[:, q * 128:(q + 1) * 128]
            return carry

        lax.fori_loop(0, h_ref.shape[0] // 384, rows, 0)

    def first(j):
        for k in range(NX):
            ref = block(j, y, k)
            if k:
                copy(j, ref, 68 + k, partner).wait_recv()
            push(j, ref, up(1, k), above)
            push(j, ref, down(1, k), below)
            push(j, ref, 32 + k, partner)

    def mine(j):
        for k in range(NX):
            copy(j, block(j, y, k, 1 - core), 32 + k, partner).wait_recv()
        project(j, [y])

    half = NY // 2

    def pieces(s):
        ups = [k for k in range(NX) if s < half or k < NX // 2]
        downs = [k for k in range(NX) if s < half or k >= NX // 2]
        return ups, downs

    def relay(j, s):
        ups, downs = pieces(s)
        for k in range(NX):
            if k in ups:
                ref = block(j, y + NY - s, k)
                copy(j, ref, up(s, k), partner).wait_recv()
                if s < half - 1 or (s == half - 1 and k < NX // 2):
                    push(j, ref, up(s + 1, k), above)
                push(j, ref, side(up(s, k)), partner)
            if k in downs:
                ref = block(j, y + s, k)
                copy(j, ref, down(s, k), partner).wait_recv()
                if s < half - 1 or (s == half - 1 and k >= NX // 2):
                    push(j, ref, down(s + 1, k), below)
                push(j, ref, side(down(s, k)), partner)

    def use(j, s):
        ups, downs = pieces(s)
        for k in ups:
            copy(j, block(j, y + NY - s, k, 1 - core), side(up(s, k)), partner).wait_recv()
        for k in downs:
            copy(j, block(j, y + s, k, 1 - core), side(down(s, k)), partner).wait_recv()
        project(j, [y + NY - s, y + s] if s < half else [y + s])

    own = [
        pltpu.make_async_copy(w_ref.at[j], block(j, y, 0), own_sem.at[j]) for j in range(2)
    ]
    for j in range(2):
        own[j].start()
    for j in range(2):
        own[j].wait()
        for k in range(1, NX):
            push(j, block(j, y, 0), 68 + k, x_peers[k - 1])
    first(0)
    mine(0)
    relay(0, 1)
    relay(0, 2)
    use(0, 1)
    relay(0, 3)
    first(1)
    use(0, 2)
    relay(0, 4)
    use(0, 3)
    use(0, 4)
    ring = Ring(pk, k_ref, plus, minus, zsend, zrecv, sent)
    ring.start()
    relay(1, 1)
    mine(1)
    ring.step(0)
    relay(1, 2)
    use(1, 1)
    ring.step(1)
    relay(1, 3)
    ring.step(2)
    use(1, 2)
    ring.step(3)
    relay(1, 4)
    ring.step(4)
    use(1, 3)
    ring.step(5)
    use(1, 4)
    ring.step(6)
    for c in sent:
        c.wait_send()


def project_keys(hidden, weights):
    tok_rows = hidden.shape[0]
    vmem = pl.BlockSpec(memory_space=pltpu.VMEM)
    return pl.pallas_call(
        project_kernel,
        name="project",
        out_shape=(
            jax.ShapeDtypeStruct((tok_rows, 128), jnp.bfloat16),
            jax.ShapeDtypeStruct((NZ, tok_rows, 128), jnp.bfloat16),
        ),
        in_specs=[vmem] * 2,
        out_specs=(vmem, vmem),
        scratch_shapes=[
            pltpu.VMEM((2, NY, 2, NX) + weights.shape[1:], jnp.bfloat16),
            pltpu.VMEM((NZ, tok_rows, 128), jnp.bfloat16),
            pltpu.SemaphoreType.DMA((2, 72)),
            pltpu.SemaphoreType.DMA((2, 72)),
            pltpu.SemaphoreType.DMA((2,)),
        ] + ring_scratch(tok_rows),
        compiler_params=pltpu.CompilerParams(collective_id=1, has_side_effects=True),
    )(hidden, weights)


def centroid_kernel(
    prior, sums_ref, cnt_ref, old_ref, pv_ref, new_ref, low_ref, v_ref,
    pair, pair_cnt, mix, mix_cnt, got, got_cnt, low, send, recv, plus, minus, zsend, zrecv
):
    me = lax.axis_index("seq")
    core = lax.rem(me, 2)
    chip = me // 2
    partner = {"seq": chip * 2 + 1 - core}
    z_up, z_down = z_neighbours()

    def peer(d):
        return {"seq": lax.rem(chip + d, CHIPS) * 2 + core}

    enter([partner, z_up, z_down], peer)

    def copy(src, dst, k, to):
        return remote(src, dst, send.at[k], recv.at[k], to)

    sent = []
    ring = Ring(pv_ref, v_ref, plus, minus, zsend, zrecv, sent)
    to_pair = copy(sums_ref.at[:, 1 - core], pair, 0, partner)
    to_pair_cnt = copy(cnt_ref.at[:, 1 - core], pair_cnt, 1, partner)
    to_pair.start()
    to_pair_cnt.start()
    ring.start()
    to_pair.wait_recv()
    to_pair_cnt.wait_recv()

    def merge(i, c):
        mix[i] = sums_ref[i, core] + pair[i]
        mix_cnt[i] = cnt_ref[i, core] + pair_cnt[i]
        return c

    lax.fori_loop(0, CHIPS, merge, 0)

    def scatter(d, c):
        to = lax.rem(chip + d, CHIPS)
        copy(mix.at[to], got.at[d - 1], 2, peer(d)).start()
        copy(mix_cnt.at[to], got_cnt.at[d - 1], 3, peer(d)).start()
        return c

    lax.fori_loop(1, CHIPS, scatter, 0)
    for s in range(3):
        ring.step(s)
    copy(got, got, 2, partner).wait_recv()
    copy(got_cnt, got_cnt, 3, partner).wait_recv()

    def add(i, c):
        return c[0] + got[i], c[1] + got_cnt[i]

    total, cnt = lax.fori_loop(0, CHIPS - 1, add, (mix[chip], mix_cnt[chip]))
    rows = total.shape[0]
    lane = lax.broadcasted_iota(jnp.int32, (rows, 128), 1)
    row = lax.broadcasted_iota(jnp.int32, (rows, 128), 0)
    count = jnp.sum(
        jnp.where(lane == row, jnp.broadcast_to(cnt, (rows, 128)), 0.0), axis=1, keepdims=True
    )
    new = (total + prior * old_ref[...]) / (count + prior)
    new_ref[...] = new
    low[core, chip] = new.astype(jnp.bfloat16)

    def gather(d, c):
        copy(low.at[core, chip], low.at[core, chip], 4, peer(d)).start()
        return c

    lax.fori_loop(1, CHIPS, gather, 0)
    for s in range(3, 6):
        ring.step(s)
    rest = low.at[core, pl.ds(0, CHIPS - 1)]
    copy(rest, rest, 4, partner).wait_recv()
    back = copy(low.at[core], low.at[core], 5, partner)
    back.start()
    ring.step(6)
    back.wait_recv()
    low_ref[:, 0] = low[0]
    low_ref[:, 1] = low[1]
    to_pair.wait_send()
    to_pair_cnt.wait_send()
    copy(got, got, 2, partner).wait_send()
    copy(got_cnt, got_cnt, 3, partner).wait_send()
    copy(rest, rest, 4, partner).wait_send()
    back.wait_send()
    for c in sent:
        c.wait_send()


def update_centroids(sums, counts, old_own, part_v, prior):
    rows, width = old_own.shape
    tok_rows = part_v.shape[1]
    vmem = pl.BlockSpec(memory_space=pltpu.VMEM)

    def body(*refs):
        centroid_kernel(prior, *refs)

    return pl.pallas_call(
        body,
        name="centroids",
        out_shape=(
            jax.ShapeDtypeStruct((rows, width), jnp.float32),
            jax.ShapeDtypeStruct((CHIPS, 2, rows, width), jnp.bfloat16),
            jax.ShapeDtypeStruct((tok_rows, 128), jnp.bfloat16),
        ),
        in_specs=[vmem] * 4,
        out_specs=(vmem, vmem, vmem),
        scratch_shapes=[
            pltpu.VMEM((CHIPS, rows, width), jnp.float32),
            pltpu.VMEM((CHIPS, 1, 128), jnp.float32),
            pltpu.VMEM((CHIPS, rows, width), jnp.float32),
            pltpu.VMEM((CHIPS, 1, 128), jnp.float32),
            pltpu.VMEM((CHIPS - 1, rows, width), jnp.float32),
            pltpu.VMEM((CHIPS - 1, 1, 128), jnp.float32),
            pltpu.VMEM((2, CHIPS, rows, width), jnp.bfloat16),
            pltpu.SemaphoreType.DMA((6,)),
            pltpu.SemaphoreType.DMA((6,)),
        ] + ring_scratch(tok_rows),
        compiler_params=pltpu.CompilerParams(collective_id=0, has_side_effects=True),
    )(sums, counts, old_own, part_v)


def shards(hidden_states, k_weight, v_weight, assignments, old_centroids):
    tok_rows = hidden_states.shape[0]
    clusters = old_centroids.shape[1]
    head_size = old_centroids.shape[2]
    n_seq = lax.axis_size("seq")
    weights = jnp.stack((k_weight.T, v_weight.T), axis=0)
    keys, part_v = project_keys(hidden_states, weights)
    onehot = assignments[0][:, None] == jnp.arange(clusters, dtype=jnp.int32)[None, :]
    local_sums = jnp.einsum(
        "tc,te->ce", onehot.astype(jnp.bfloat16), keys, preferred_element_type=jnp.float32
    )
    local_counts = jnp.sum(onehot.astype(jnp.float32), axis=0)
    prior_weight = float(tok_rows * n_seq // clusters)
    share = clusters // n_seq
    counts = jnp.pad(
        local_counts.reshape(CHIPS, 2, 1, share), ((0, 0), (0, 0), (0, 0), (0, 128 - share))
    )
    old_own = lax.dynamic_slice_in_dim(old_centroids[0], lax.axis_index("seq") * share, share, 0)
    new_own, low, value_cache = update_centroids(
        local_sums.reshape(CHIPS, 2, share, head_size), counts, old_own, part_v, prior_weight
    )
    low = low.reshape(clusters, head_size)
    wide = low.astype(jnp.float32)
    centroid_square = jnp.sum(wide * wide, axis=1)
    key_wide = keys.astype(jnp.float32)
    key_square = jnp.sum(key_wide * key_wide, axis=1)
    cross_term = jnp.einsum("te,ce->tc", keys, low, preferred_element_type=jnp.float32)
    dist = (key_square[:, None] - 2.0 * cross_term + centroid_square[None, :]) / head_size
    return (keys, value_cache, new_own[None], dist.astype(jnp.bfloat16)[None])


def solution(mesh):
    in_specs = (
        P("seq", "head"),
        P("head", "seq"),
        P("head", "seq"),
        P("head", "seq"),
        P("head", None, None),
    )
    out_specs = (P("seq", "head"), P("seq", "head"), P("head", "seq", None), P("head", "seq", None))
    return jax.shard_map(shards, mesh=mesh, in_specs=in_specs, out_specs=out_specs, check_vma=False)
```

```python
import jax
import jax.numpy as jnp
from jax import lax
from jax.experimental import pallas as pl
from jax.experimental.pallas import tpu as pltpu
from jax.sharding import PartitionSpec as P

MESH = pl.DeviceIdType.MESH
NX, NY, NZ = 4, 8, 8
CHIPS = NX * NY
PIECES = 2


def remote(src, dst, send_sem, recv_sem, to):
    return pltpu.make_async_remote_copy(
        src_ref=src, dst_ref=dst, send_sem=send_sem, recv_sem=recv_sem,
        device_id=to, device_id_type=MESH,
    )


def z_neighbours():
    z = lax.axis_index("head")
    return {"head": lax.rem(z + 1, NZ)}, {"head": lax.rem(z + NZ - 1, NZ)}


class Ring:
    def __init__(self, part, out, plus, minus, send, recv, sent):
        self.part, self.out, self.send, self.recv, self.sent = part, out, send, recv, sent
        self.z = lax.axis_index("head")
        up, down = z_neighbours()
        self.half = out.shape[0] // 2
        self.tall = self.half // PIECES
        self.ways = ((0, plus, up, NZ - 1), (1, minus, down, 1))

    def copy(self, src, dst, i, to):
        return remote(src, dst, self.send.at[i], self.recv.at[i], to)

    def push(self, src, dst, i, to):
        c = self.copy(src, dst, i, to)
        c.start()
        self.sent.append(c)

    def start(self):
        for p in range(PIECES):
            for j, slots, to, step in self.ways:
                src = self.part.at[
                    lax.rem(self.z + step, NZ), pl.ds(j * self.half + p * self.tall, self.tall)
                ]
                dst = slots.at[0, pl.ds(p * self.tall, self.tall)]
                self.push(src, dst, j * (NZ - 1) * PIECES + p, to)

    def step(self, s):
        for p in range(PIECES):
            rows = pl.ds(p * self.tall, self.tall)
            for j, slots, to, step in self.ways:
                i = (j * (NZ - 1) + s) * PIECES + p
                here = slots.at[s, rows]
                full = pl.ds(j * self.half + p * self.tall, self.tall)
                self.copy(here, here, i, to).wait_recv()
                head = lax.rem(self.z + step * (s + 2), NZ)
                total = slots[s, rows].astype(jnp.float32) + self.part[head, full].astype(jnp.float32)
                total = total.astype(jnp.bfloat16)
                if s < NZ - 2:
                    slots[s, rows] = total
                    self.push(here, slots.at[s + 1, rows], i + PIECES, to)
                else:
                    self.out[full, :] = total


def ring_scratch(tok_rows):
    n_ring = 2 * (NZ - 1) * PIECES
    return [
        pltpu.VMEM((NZ - 1, tok_rows // 2, 128), jnp.bfloat16),
        pltpu.VMEM((NZ - 1, tok_rows // 2, 128), jnp.bfloat16),
        pltpu.SemaphoreType.DMA((n_ring,)),
        pltpu.SemaphoreType.DMA((n_ring,)),
    ]


def enter(peers, chips=None):
    barrier = pltpu.get_barrier_semaphore()
    for peer in peers:
        pl.semaphore_signal(barrier, inc=1, device_id=peer, device_id_type=MESH)
    count = len(peers)
    if chips is not None:

        def greet(d, c):
            pl.semaphore_signal(barrier, inc=1, device_id=chips(d), device_id_type=MESH)
            return c

        lax.fori_loop(1, CHIPS, greet, 0)
        count += CHIPS - 1
    pl.semaphore_wait(barrier, count)


def project_kernel(
    h_ref, w_ref, k_ref, pv_ref, held, pk, send, recv, own_sem, plus, minus, zsend, zrecv
):
    me = lax.axis_index("seq")
    core = lax.rem(me, 2)
    x = lax.rem(me // 2, NX)
    y = me // (2 * NX)

    def at(y_, x_, core_):
        return {"seq": (lax.rem(y_, NY) * NX + lax.rem(x_, NX)) * 2 + core_}

    above, below = at(y + 1, x, core), at(y + NY - 1, x, core)
    partner = at(y, x, 1 - core)
    z_up, z_down = z_neighbours()
    x_peers = [at(y, x + NX - k, core) for k in range(1, NX)]
    enter([above, below, partner, z_up, z_down] + x_peers)

    sent = []
    parts = (pk, pv_ref)

    def block(j, row, k, c=core):
        return held.at[j, lax.rem(row, NY), c, lax.rem(x + k, NX)]

    def copy(j, ref, i, to):
        return remote(ref, ref, send.at[j, i], recv.at[j, i], to)

    def push(j, ref, i, to):
        c = copy(j, ref, i, to)
        c.start()
        sent.append(c)

    def up(s, k):
        return (s - 1) * NX + k

    def down(s, k):
        return 16 + (s - 1) * NX + k

    def side(i):
        return 36 + i

    def project(j, rows_y):
        heads = [lax.rem(row, NY) for row in rows_y]
        weights = jnp.concatenate(
            [held[j, head, c, i] for head in heads for i in range(NX) for c in range(2)], axis=0
        )

        def rows(i, carry):
            at_rows = pl.ds(pl.multiple_of(i * 384, 384), 384)
            out = lax.dot_general(
                h_ref[at_rows, :], weights, (((1,), (1,)), ((), ())),
                preferred_element_type=jnp.float32,
            ).astype(jnp.bfloat16)
            for q, head in enumerate(heads):
                parts[j][head, at_rows, :] = out[:, q * 128:(q + 1) * 128]
            return carry

        lax.fori_loop(0, h_ref.shape[0] // 384, rows, 0)

    def first(j):
        for k in range(NX):
            ref = block(j, y, k)
            if k:
                copy(j, ref, 68 + k, partner).wait_recv()
            push(j, ref, up(1, k), above)
            push(j, ref, down(1, k), below)
            push(j, ref, 32 + k, partner)

    def mine(j):
        for k in range(NX):
            copy(j, block(j, y, k, 1 - core), 32 + k, partner).wait_recv()
        project(j, [y])

    half = NY // 2

    def pieces(s):
        ups = [k for k in range(NX) if s < half or k < NX // 2]
        downs = [k for k in range(NX) if s < half or k >= NX // 2]
        return ups, downs

    def relay(j, s):
        ups, downs = pieces(s)
        for k in range(NX):
            if k in ups:
                ref = block(j, y + NY - s, k)
                copy(j, ref, up(s, k), partner).wait_recv()
                if s < half - 1 or (s == half - 1 and k < NX // 2):
                    push(j, ref, up(s + 1, k), above)
                push(j, ref, side(up(s, k)), partner)
            if k in downs:
                ref = block(j, y + s, k)
                copy(j, ref, down(s, k), partner).wait_recv()
                if s < half - 1 or (s == half - 1 and k >= NX // 2):
                    push(j, ref, down(s + 1, k), below)
                push(j, ref, side(down(s, k)), partner)

    def use(j, s):
        ups, downs = pieces(s)
        for k in ups:
            copy(j, block(j, y + NY - s, k, 1 - core), side(up(s, k)), partner).wait_recv()
        for k in downs:
            copy(j, block(j, y + s, k, 1 - core), side(down(s, k)), partner).wait_recv()
        project(j, [y + NY - s, y + s] if s < half else [y + s])

    own = [
        pltpu.make_async_copy(w_ref.at[j], block(j, y, 0), own_sem.at[j]) for j in range(2)
    ]
    for j in range(2):
        own[j].start()
    for j in range(2):
        own[j].wait()
        for k in range(1, NX):
            push(j, block(j, y, 0), 68 + k, x_peers[k - 1])
    first(0)
    mine(0)
    relay(0, 1)
    relay(0, 2)
    first(1)
    use(0, 1)
    relay(0, 3)
    use(0, 2)
    relay(0, 4)
    use(0, 3)
    use(0, 4)
    ring = Ring(pk, k_ref, plus, minus, zsend, zrecv, sent)
    ring.start()
    relay(1, 1)
    mine(1)
    ring.step(0)
    relay(1, 2)
    use(1, 1)
    ring.step(1)
    relay(1, 3)
    ring.step(2)
    use(1, 2)
    ring.step(3)
    relay(1, 4)
    ring.step(4)
    use(1, 3)
    ring.step(5)
    use(1, 4)
    ring.step(6)
    for c in sent:
        c.wait_send()


def project_keys(hidden, weights):
    tok_rows = hidden.shape[0]
    vmem = pl.BlockSpec(memory_space=pltpu.VMEM)
    return pl.pallas_call(
        project_kernel,
        name="project",
        out_shape=(
            jax.ShapeDtypeStruct((tok_rows, 128), jnp.bfloat16),
            jax.ShapeDtypeStruct((NZ, tok_rows, 128), jnp.bfloat16),
        ),
        in_specs=[vmem] * 2,
        out_specs=(vmem, vmem),
        scratch_shapes=[
            pltpu.VMEM((2, NY, 2, NX) + weights.shape[1:], jnp.bfloat16),
            pltpu.VMEM((NZ, tok_rows, 128), jnp.bfloat16),
            pltpu.SemaphoreType.DMA((2, 72)),
            pltpu.SemaphoreType.DMA((2, 72)),
            pltpu.SemaphoreType.DMA((2,)),
        ] + ring_scratch(tok_rows),
        compiler_params=pltpu.CompilerParams(collective_id=1, has_side_effects=True),
    )(hidden, weights)


def centroid_kernel(
    prior, sums_ref, cnt_ref, old_ref, pv_ref, new_ref, low_ref, v_ref,
    pair, pair_cnt, mix, mix_cnt, got, got_cnt, low, send, recv, plus, minus, zsend, zrecv
):
    me = lax.axis_index("seq")
    core = lax.rem(me, 2)
    chip = me // 2
    partner = {"seq": chip * 2 + 1 - core}
    z_up, z_down = z_neighbours()

    def peer(d):
        return {"seq": lax.rem(chip + d, CHIPS) * 2 + core}

    enter([partner, z_up, z_down], peer)

    def copy(src, dst, k, to):
        return remote(src, dst, send.at[k], recv.at[k], to)

    sent = []
    ring = Ring(pv_ref, v_ref, plus, minus, zsend, zrecv, sent)
    to_pair = copy(sums_ref.at[:, 1 - core], pair, 0, partner)
    to_pair_cnt = copy(cnt_ref.at[:, 1 - core], pair_cnt, 1, partner)
    to_pair.start()
    to_pair_cnt.start()
    ring.start()
    to_pair.wait_recv()
    to_pair_cnt.wait_recv()

    def merge(i, c):
        mix[i] = sums_ref[i, core] + pair[i]
        mix_cnt[i] = cnt_ref[i, core] + pair_cnt[i]
        return c

    lax.fori_loop(0, CHIPS, merge, 0)

    def scatter(d, c):
        to = lax.rem(chip + d, CHIPS)
        copy(mix.at[to], got.at[d - 1], 2, peer(d)).start()
        copy(mix_cnt.at[to], got_cnt.at[d - 1], 3, peer(d)).start()
        return c

    lax.fori_loop(1, CHIPS, scatter, 0)
    for s in range(3):
        ring.step(s)
    copy(got, got, 2, partner).wait_recv()
    copy(got_cnt, got_cnt, 3, partner).wait_recv()

    def add(i, c):
        return c[0] + got[i], c[1] + got_cnt[i]

    total, cnt = lax.fori_loop(0, CHIPS - 1, add, (mix[chip], mix_cnt[chip]))
    rows = total.shape[0]
    lane = lax.broadcasted_iota(jnp.int32, (rows, 128), 1)
    row = lax.broadcasted_iota(jnp.int32, (rows, 128), 0)
    count = jnp.sum(
        jnp.where(lane == row, jnp.broadcast_to(cnt, (rows, 128)), 0.0), axis=1, keepdims=True
    )
    new = (total + prior * old_ref[...]) / (count + prior)
    new_ref[...] = new
    low[core, chip] = new.astype(jnp.bfloat16)

    def gather(d, c):
        copy(low.at[core, chip], low.at[core, chip], 4, peer(d)).start()
        return c

    lax.fori_loop(1, CHIPS, gather, 0)
    for s in range(3, 6):
        ring.step(s)
    rest = low.at[core, pl.ds(0, CHIPS - 1)]
    copy(rest, rest, 4, partner).wait_recv()
    back = copy(low.at[core], low.at[core], 5, partner)
    back.start()
    ring.step(6)
    back.wait_recv()
    low_ref[:, 0] = low[0]
    low_ref[:, 1] = low[1]
    to_pair.wait_send()
    to_pair_cnt.wait_send()
    copy(got, got, 2, partner).wait_send()
    copy(got_cnt, got_cnt, 3, partner).wait_send()
    copy(rest, rest, 4, partner).wait_send()
    back.wait_send()
    for c in sent:
        c.wait_send()


def update_centroids(sums, counts, old_own, part_v, prior):
    rows, width = old_own.shape
    tok_rows = part_v.shape[1]
    vmem = pl.BlockSpec(memory_space=pltpu.VMEM)

    def body(*refs):
        centroid_kernel(prior, *refs)

    return pl.pallas_call(
        body,
        name="centroids",
        out_shape=(
            jax.ShapeDtypeStruct((rows, width), jnp.float32),
            jax.ShapeDtypeStruct((CHIPS, 2, rows, width), jnp.bfloat16),
            jax.ShapeDtypeStruct((tok_rows, 128), jnp.bfloat16),
        ),
        in_specs=[vmem] * 4,
        out_specs=(vmem, vmem, vmem),
        scratch_shapes=[
            pltpu.VMEM((CHIPS, rows, width), jnp.float32),
            pltpu.VMEM((CHIPS, 1, 128), jnp.float32),
            pltpu.VMEM((CHIPS, rows, width), jnp.float32),
            pltpu.VMEM((CHIPS, 1, 128), jnp.float32),
            pltpu.VMEM((CHIPS - 1, rows, width), jnp.float32),
            pltpu.VMEM((CHIPS - 1, 1, 128), jnp.float32),
            pltpu.VMEM((2, CHIPS, rows, width), jnp.bfloat16),
            pltpu.SemaphoreType.DMA((6,)),
            pltpu.SemaphoreType.DMA((6,)),
        ] + ring_scratch(tok_rows),
        compiler_params=pltpu.CompilerParams(collective_id=0, has_side_effects=True),
    )(sums, counts, old_own, part_v)


def shards(hidden_states, k_weight, v_weight, assignments, old_centroids):
    tok_rows = hidden_states.shape[0]
    clusters = old_centroids.shape[1]
    head_size = old_centroids.shape[2]
    n_seq = lax.axis_size("seq")
    weights = jnp.stack((k_weight.T, v_weight.T), axis=0)
    keys, part_v = project_keys(hidden_states, weights)
    onehot = assignments[0][:, None] == jnp.arange(clusters, dtype=jnp.int32)[None, :]
    local_sums = jnp.einsum(
        "tc,te->ce", onehot.astype(jnp.bfloat16), keys, preferred_element_type=jnp.float32
    )
    local_counts = jnp.sum(onehot.astype(jnp.float32), axis=0)
    prior_weight = float(tok_rows * n_seq // clusters)
    share = clusters // n_seq
    counts = jnp.pad(
        local_counts.reshape(CHIPS, 2, 1, share), ((0, 0), (0, 0), (0, 0), (0, 128 - share))
    )
    old_own = lax.dynamic_slice_in_dim(old_centroids[0], lax.axis_index("seq") * share, share, 0)
    new_own, low, value_cache = update_centroids(
        local_sums.reshape(CHIPS, 2, share, head_size), counts, old_own, part_v, prior_weight
    )
    low = low.reshape(clusters, head_size)
    wide = low.astype(jnp.float32)
    centroid_square = jnp.sum(wide * wide, axis=1)
    key_wide = keys.astype(jnp.float32)
    key_square = jnp.sum(key_wide * key_wide, axis=1)
    cross_term = jnp.einsum("te,ce->tc", keys, low, preferred_element_type=jnp.float32)
    dist = (key_square[:, None] - 2.0 * cross_term + centroid_square[None, :]) / head_size
    return (keys, value_cache, new_own[None], dist.astype(jnp.bfloat16)[None])


def solution(mesh):
    in_specs = (
        P("seq", "head"),
        P("head", "seq"),
        P("head", "seq"),
        P("head", "seq"),
        P("head", None, None),
    )
    out_specs = (P("seq", "head"), P("seq", "head"), P("head", "seq", None), P("head", "seq", None))
    return jax.shard_map(shards, mesh=mesh, in_specs=in_specs, out_specs=out_specs, check_vma=False)
```
